32 devices in a mesh: groups: 2 (over x), sample: 16 (over z, y, core).
Axes of the slice: x: 2, y: 2, z: 4, core: 2. Of those that a mesh axis runs over, the one named last changes fastest.
Arguments:
- prompt_states: bfloat16 [16384, 8192], P(('groups', 'sample')), parts along dimension 0, may hold values from -6 to 6
- page_table: int32 [128], P('groups'), parts along dimension 0, may hold values from 0 to 63, each once
- step_states: bfloat16 [2, 64, 8192], P(None, 'groups'), parts along dimension 1, may hold values from -15 to 15
- sample_order: int32 [64], P('groups'), parts along dimension 0, may hold values from 0 to 31, each once
- key_weight: bfloat16 [8192, 512], P('sample'), may hold values from -0.088388348 to 0.088388348
- value_weight: bfloat16 [8192, 512], P('sample'), may hold values from -0.0625 to 0.0625
- query_weight: bfloat16 [8192, 4096], P(None, 'sample'), may hold values from -0.121533978 to 0.121533978
- out_weight: bfloat16 [4096, 8192], P('sample'), may hold values from -0.125 to 0.125
Outputs:
- attn_out: bfloat16 [2, 64, 8192], P(None, 'groups', 'sample'), parts along dimension 1
The draws below stay inside these ranges and needn't reach their ends.
There are 2 independent parts, one for each index of `groups`. The reference program is written for one: setup_inputs(seed, part) draws one part's arguments, and reference() takes and returns one part's arrays. A program takes and returns all parts, laid end to end along the dimension named above; an argument that names none is the same for every part. Nothing has to cross between parts.
Inputs may be any that keep to these rules, and one draw needn't show every extreme that they name: `page_table`: A permutation: entry p * 64 + j is the physical page that holds logical page j of prompt p; physical page r is rows r * 128 to (r + 1) * 128 - 1 of prompt_states. `sample_order`: A permutation; completion i continues prompt sample_order[i] // 32.
All inputs are finite; a program needn't handle non-finite values.
Results may differ from the reference program's by a relative error of at most 0.034.
Values may be sent and summed in bfloat16 or wider, within the bound.
A program may use at most 128 MiB of HBM per device.

```python
import jax
import jax.numpy as jnp
from jax import lax

D = 8192
HEAD_DIM = 128
HEADS = 32
KV_HEADS = 4
GQA = 8
PAGE = 128
PROMPT_PAGES = 64
GROUP = 32
PAGES = 64
PROMPTS = 1
PROMPT_LEN = 8192
SAMPLES = 32
N_SAMPLE = 16


def weight_pair(key):
    base_part = jnp.clip(jax.random.normal(jax.random.fold_in(key, 31), (D, KV_HEADS, 1, HEAD_DIM), jnp.float32), -5.0, 5.0)
    base_part = base_part * (1.6 / D ** 0.5)
    noise_part = jnp.clip(jax.random.normal(jax.random.fold_in(key, 32), (D, KV_HEADS, GQA, HEAD_DIM), jnp.float32), -5.0, 5.0)
    noise_part = noise_part * (1.45 / D ** 0.5)
    query_part = 0.42 * base_part + noise_part
    return (base_part.reshape(D, KV_HEADS * HEAD_DIM), query_part.reshape(D, HEADS * HEAD_DIM))


def draw_key_weight(key, part):
    return weight_pair(key)[0].astype(jnp.bfloat16)


def draw_query_weight(key, part):
    return weight_pair(key)[1].astype(jnp.bfloat16)


def draw_step_states(key, part):
    first_part = jnp.clip(jax.random.normal(jax.random.fold_in(key, 41), (SAMPLES, D), jnp.float32), -5.0, 5.0)
    fresh_part = jnp.clip(jax.random.normal(jax.random.fold_in(key, 42), (SAMPLES, D), jnp.float32), -5.0, 5.0)
    second_part = 0.8 * first_part + 0.6 * fresh_part
    return jnp.stack([first_part, second_part]).astype(jnp.bfloat16)


def spiked(result, rng, source, target, shards_of, factor):
    owner, partner = [(jnp.arange(result.shape[axis_at]) // (result.shape[axis_at] // shards_of)).reshape([-1 if axis == axis_at else 1 for axis in range(result.ndim)]) for axis_at in (source, target)]
    chosen = jax.random.permutation(rng, shards_of)[partner]
    strong = (owner == chosen) | (owner == (partner + shards_of // 2) % shards_of)
    return jnp.where(strong, factor * result, result)


def levels(own_key, shape, split, smallest, largest):
    def one(axis_at, parts):
        heights = jax.random.uniform(jax.random.fold_in(jax.random.fold_in(own_key, 6), axis_at), (parts,), jnp.float32, smallest / len(split), largest / len(split))
        return jnp.repeat(jnp.exp(heights), shape[axis_at] // parts).reshape((-1,) + (1,) * (len(shape) - axis_at - 1))

    level = one(*split[0])
    for cut in split[1:]:
        level = level * one(*cut)
    return level


def noise(rng, shape, width, most, split=(), held_as=jnp.bfloat16):
    level = levels(rng, shape, split, -0.22, 0.18) if split else 1.0
    values = jax.random.normal(rng, shape, jnp.float32) * width * level
    return jnp.minimum(jnp.maximum(values, -most), most).astype(held_as)


def gaussian_with(stream_key, shape, width, most, split, heavy, kind=jnp.bfloat16):
    entries = width * jax.random.normal(stream_key, shape, jnp.float32)
    if split:
        entries = entries * levels(stream_key, shape, split, -0.22, 0.18)
    return jnp.clip(spiked(entries, jax.random.fold_in(stream_key, 3), *heavy), -most, most).astype(kind)


def setup_inputs(seed: int = 0, part: int = 0) -> dict:
    arg_keys = jax.random.split(jax.random.key(seed), 9)
    part_splits = jax.random.split(jax.random.fold_in(arg_keys[8], part), 9)
    prompt_states = noise(part_splits[0], (PAGES * PAGE, D), 1.0, 6.0, ((0, 16),))
    page_table = jax.random.permutation(part_splits[1], PAGES).astype(jnp.int32)
    step_states = draw_step_states(jax.random.fold_in(jax.random.fold_in(arg_keys[8], part), 71), part)
    sample_order = jax.random.permutation(part_splits[3], SAMPLES).astype(jnp.int32)
    key_weight = draw_key_weight(jax.random.fold_in(arg_keys[8], 71), part)
    value_weight = noise(arg_keys[5], (D, KV_HEADS * HEAD_DIM), D ** -0.5, 0.0625, ((0, 16),))
    query_weight = draw_query_weight(jax.random.fold_in(arg_keys[8], 71), part)
    out_weight = gaussian_with(arg_keys[7], (HEADS * HEAD_DIM, D), (HEADS * HEAD_DIM) ** -0.5, 0.125, ((0, 16),), (0, 1, 16, 2.0))
    return {"prompt_states": prompt_states, "page_table": page_table, "step_states": step_states, "sample_order": sample_order, "key_weight": key_weight, "value_weight": value_weight, "query_weight": query_weight, "out_weight": out_weight}


rope_base = 1000000.0


def rotate(vector, position):
    half_dim = vector.shape[-1] // 2
    frequency = rope_base ** (-jnp.arange(half_dim, dtype=jnp.float32) * 2.0 / vector.shape[-1])
    angles = position.astype(jnp.float32)[..., None] * frequency
    cosine = jnp.cos(angles)
    sine_part = jnp.sin(angles)
    first_half = vector[..., :half_dim]
    second_half = vector[..., half_dim:]
    return jnp.concatenate([first_half * cosine - second_half * sine_part, second_half * cosine + first_half * sine_part], axis=-1)


def finish_heads(prefix_top, prefix_total, prefix_sum, queries, new_keys, new_values):
    score_scale = queries.shape[-1] ** -0.5
    query_wide = queries.astype(jnp.float32)
    key_wide = new_keys.astype(jnp.float32)
    value_wide = new_values.astype(jnp.float32)
    own_score = jnp.sum(query_wide * key_wide, axis=-1) * score_scale
    back_score = jnp.sum(query_wide[1] * key_wide[0], axis=-1) * score_scale
    first_high = jnp.maximum(prefix_top[0], own_score[0])
    first_old = jnp.exp(prefix_top[0] - first_high)
    first_own = jnp.exp(own_score[0] - first_high)
    first_out = (first_old[..., None] * prefix_sum[0] + first_own[..., None] * value_wide[0]) / (first_old * prefix_total[0] + first_own)[..., None]
    second_high = jnp.maximum(jnp.maximum(prefix_top[1], own_score[1]), back_score)
    second_old = jnp.exp(prefix_top[1] - second_high)
    second_back = jnp.exp(back_score - second_high)
    second_own = jnp.exp(own_score[1] - second_high)
    second_num = second_old[..., None] * prefix_sum[1] + second_back[..., None] * value_wide[0] + second_own[..., None] * value_wide[1]
    second_out = second_num / (second_old * prefix_total[1] + second_back + second_own)[..., None]
    return jnp.stack([first_out, second_out]).astype(jnp.bfloat16)


def reference(prompt_states, page_table, step_states, sample_order, key_weight, value_weight, query_weight, out_weight):
    score_scale = HEAD_DIM ** -0.5
    page_rows = prompt_states.reshape(PAGES, PAGE, D)
    logical = page_table.reshape(PROMPTS, PROMPT_PAGES)
    token_place = jnp.arange(PROMPT_LEN, dtype=jnp.int32)

    def prefill(prompt):
        states = page_rows[logical[prompt]].reshape(PROMPT_LEN, D)
        keys = jnp.dot(states, key_weight, preferred_element_type=jnp.float32).reshape(PROMPT_LEN, KV_HEADS, HEAD_DIM)
        keys = rotate(keys, token_place[:, None]).astype(jnp.bfloat16)
        values = jnp.dot(states, value_weight, preferred_element_type=jnp.float32).astype(jnp.bfloat16)
        return keys, values.reshape(PROMPT_LEN, KV_HEADS, HEAD_DIM)

    prefix_keys, prefix_values = lax.map(prefill, jnp.arange(PROMPTS, dtype=jnp.int32))
    flat_states = step_states.reshape(2 * SAMPLES, D)
    step_place = (PROMPT_LEN + jnp.arange(2, dtype=jnp.int32))[:, None, None]
    queries = jnp.dot(flat_states, query_weight, preferred_element_type=jnp.float32).reshape(2, SAMPLES, HEADS, HEAD_DIM)
    queries = rotate(queries, step_place).astype(jnp.bfloat16)
    new_keys = jnp.dot(flat_states, key_weight, preferred_element_type=jnp.float32).reshape(2, SAMPLES, KV_HEADS, HEAD_DIM)
    new_keys = rotate(new_keys, step_place).astype(jnp.bfloat16)
    new_values = jnp.dot(flat_states, value_weight, preferred_element_type=jnp.float32).astype(jnp.bfloat16)
    new_values = new_values.reshape(2, SAMPLES, KV_HEADS, HEAD_DIM)
    inverse = jnp.zeros((SAMPLES,), jnp.int32).at[sample_order].set(jnp.arange(SAMPLES, dtype=jnp.int32))
    grouped = queries[:, inverse].reshape(2, PROMPTS, GROUP, KV_HEADS, GQA, HEAD_DIM)

    def attend(prompt):
        block_query = grouped[:, prompt].astype(jnp.float32)
        keys = prefix_keys[prompt].astype(jnp.float32)
        values = prefix_values[prompt].astype(jnp.float32)
        scores = jnp.einsum("smcgd,lcd->smcgl", block_query, keys) * score_scale
        prefix_top = jnp.max(scores, axis=-1)
        weights = jnp.exp(scores - prefix_top[..., None])
        prefix_total = jnp.sum(weights, axis=-1)
        rounded = lax.optimization_barrier(weights.astype(jnp.bfloat16)).astype(jnp.float32)
        prefix_sum = jnp.einsum("smcgl,lcd->smcgd", rounded, values)
        return prefix_top, prefix_total, prefix_sum

    prefix_top, prefix_total, prefix_sum = lax.map(attend, jnp.arange(PROMPTS, dtype=jnp.int32))
    prefix_top = jnp.moveaxis(prefix_top, 0, 1).reshape(2, SAMPLES, HEADS)[:, sample_order]
    prefix_total = jnp.moveaxis(prefix_total, 0, 1).reshape(2, SAMPLES, HEADS)[:, sample_order]
    prefix_sum = jnp.moveaxis(prefix_sum, 0, 1).reshape(2, SAMPLES, HEADS, HEAD_DIM)[:, sample_order]
    head_out = finish_heads(prefix_top, prefix_total, prefix_sum, queries, jnp.repeat(new_keys, GQA, axis=2), jnp.repeat(new_values, GQA, axis=2))
    flat_out = head_out.reshape(2 * SAMPLES, HEADS * HEAD_DIM)
    block_width = (HEADS // N_SAMPLE) * HEAD_DIM

    def add_block(running, block):
        start_col = (block * block_width).astype(jnp.int32)
        piece = lax.dynamic_slice_in_dim(flat_out, start_col, block_width, 1)
        weight_rows = lax.dynamic_slice_in_dim(out_weight, start_col, block_width, 0)
        term = jnp.dot(piece, weight_rows, preferred_element_type=jnp.float32).astype(jnp.bfloat16)
        term = lax.optimization_barrier(term).astype(jnp.float32)
        return running + term, None

    total_out, unused = lax.scan(add_block, jnp.zeros((2 * SAMPLES, D), jnp.float32), jnp.arange(N_SAMPLE, dtype=jnp.int32))
    return total_out.astype(jnp.bfloat16).reshape(2, SAMPLES, D)
```

```python
import functools

import jax
import jax.numpy as jnp
from jax import lax
from jax.experimental import pallas as pl
from jax.experimental.pallas import tpu as pltpu
from jax.sharding import PartitionSpec as P

HEAD_DIM = 128
KV_HEADS = 4
GQA = 8
PAGE = 128
PROMPT_PAGES = 64
HALF = KV_HEADS // 2 * HEAD_DIM
LOW = -1e30
TAIL = 16
MESH = pl.DeviceIdType.MESH
ROPE_BASE = 1000000.0


def flip(value, bits):
    result, weight = value, 1
    while weight <= bits:
        if bits & weight:
            result = result + weight * (1 - 2 * lax.rem(lax.div(value, weight), 2))
        weight *= 2
    return result


def turn(value, cosine, sine):
    return value * cosine + pltpu.roll(value, HEAD_DIM // 2, 1) * sine


def kernel(cfg, *refs):
    groups, devices, near, samples, heads, masked = cfg
    (states, step, wk, wv, wq, wo, cosine, sine) = refs[:8]
    refs = refs[8:]
    if masked:
        token_prompt, query_prompt = refs[:2]
        refs = refs[2:]
    (out, st, wbuf, wqb, wob, acc, kb, vb, qown, qbuf, pout, pbuf, nk, nkr, tbuf, prbuf, sbuf, rbuf,
     load_sem, send_sem, wsem, st_sem, qsem, psem, nsem, pair_sem, rsem) = refs
    chips = devices // 2
    deep = chips // near
    rows = wk.shape[0]
    part = 2 * rows // groups
    own_parts = groups // 2
    tokens_here = states.shape[0]
    tokens = 2 * tokens_here
    wide = step.shape[0]
    dim = step.shape[1]
    cols = dim // devices
    half = devices // 2

    g = lax.axis_index("groups")
    me = lax.axis_index("sample")
    c = lax.rem(me, 2)
    p = lax.div(me, 2)
    y = lax.rem(p, near)
    z = lax.div(p, near)
    mate = p * 2 + 1 - c
    kv = lax.div(me * heads, GQA)
    kv_core = lax.div(kv, 2)
    kv_slot = lax.rem(kv, 2)

    def aligned(value, step_size):
        return pl.multiple_of(value, step_size)

    my_rows = pl.ds(aligned(c * tokens_here, tokens_here), tokens_here)
    loads = [
        pltpu.make_async_copy(step, st.at[pl.ds(tokens, wide)], load_sem.at[0]),
        pltpu.make_async_copy(wq, wqb, load_sem.at[1]),
        pltpu.make_async_copy(states, st.at[my_rows], load_sem.at[2]),
        pltpu.make_async_copy(wo, wob, load_sem.at[3]),
    ]
    own_w = pl.ds(aligned(me * rows, rows), rows)
    own_cols = pl.ds(aligned(c * HALF, HALF), HALF)
    loads.append(
        pltpu.make_async_copy(wk.at[:, own_cols], wbuf.at[own_w, pl.ds(0, HALF)], load_sem.at[4])
    )
    loads.append(
        pltpu.make_async_copy(wv.at[:, own_cols], wbuf.at[own_w, pl.ds(HALF, HALF)], load_sem.at[5])
    )
    for load in loads:
        load.start()

    barrier = pltpu.get_barrier_semaphore()
    for k in range(1, devices):
        pl.semaphore_signal(
            barrier, inc=1, device_id=(g, flip(me, k)), device_id_type=MESH
        )
    for k in range(1, groups):
        pl.semaphore_signal(
            barrier, inc=1, device_id=(lax.rem(g + k, groups), me), device_id_type=MESH
        )
    pl.semaphore_wait(barrier, devices + groups - 2)

    sends = []

    def send(src, dst, sem, target, when=None):
        copy = pltpu.make_async_remote_copy(
            src_ref=src, dst_ref=dst, send_sem=send_sem.at[len(sends)], recv_sem=sem,
            device_id=target, device_id_type=MESH,
        )
        if when is None:
            copy.start()
        else:
            pl.when(when)(copy.start)
        sends.append((copy, when))

    def w_rows(block):
        return pl.ds(aligned(block * part, part), part)

    def send_own(src_row, block, core, target, when=None):
        src_rows = pl.ds(src_row, part)
        src_cols = pl.ds(aligned(core * HALF, HALF), HALF)
        send(wk.at[src_rows, src_cols], wbuf.at[w_rows(block), pl.ds(0, HALF)],
             wsem.at[block], target, when)
        send(wv.at[src_rows, src_cols], wbuf.at[w_rows(block), pl.ds(HALF, HALF)],
             wsem.at[block], target, when)

    def w_wait(block):
        view = wbuf.at[w_rows(block)]
        pltpu.make_async_copy(view, view, wsem.at[block]).wait()

    owner = lax.div(g, own_parts)
    line_row = aligned(lax.rem(g, own_parts) * part, part)
    line_block = p * groups + g
    for k in range(1, deep):
        chip = flip(z, k) * near + y
        for core in range(2):
            send_own(line_row, line_block, core, (g, chip * 2 + core), c == owner)
    for h in range(own_parts):
        block = p * groups + c * own_parts + h
        for k in range(1, near):
            chip = z * near + flip(y, k)
            for core in range(2):
                send_own(h * part, block, core, (g, chip * 2 + core))
        send_own(h * part, block, 1 - c, (g, mate))
    send(states, st.at[my_rows], st_sem, (g, mate))

    loads[0].wait()
    loads[1].wait()
    depth = 1024

    def q_step(i, total):
        at = pl.ds(aligned(i * depth, depth), depth)
        return total + jnp.dot(
            st[pl.ds(tokens, wide), at], wqb[at, :], preferred_element_type=jnp.float32
        )

    queries = lax.fori_loop(
        0, dim // depth, q_step, jnp.zeros((wide, heads * HEAD_DIM), jnp.float32)
    )
    step_cos = cosine[pl.ds(tokens, wide), :]
    step_sin = sine[pl.ds(tokens, wide), :]
    for h in range(heads):
        one = queries[:, h * HEAD_DIM : (h + 1) * HEAD_DIM]
        qown[pl.ds(h * wide, wide), :] = turn(one, step_cos, step_sin).astype(jnp.bfloat16)

    def give(src, dst, sem, target):
        send(src, dst, sem, (g, target), target != me)

        @pl.when(target == me)
        def _():
            pltpu.make_async_copy(src, dst, sem).start()

    q_slot = lax.rem(me, half)
    for k in range(chips):
        give(qown, qbuf.at[q_slot], qsem.at[q_slot], flip(p, k) * 2 + kv_core)

    def cross(block):
        view = wbuf.at[w_rows(block)]
        for k in range(1, groups):
            send(view, view, wsem.at[block], (lax.rem(g + k, groups), me))

    def second(k):
        for j in range(1, near):
            block = (flip(z, k) * near + flip(y, j)) * groups + g
            w_wait(block)
            cross(block)

    for k in range(1, deep):
        block = (flip(z, k) * near + y) * groups + g
        w_wait(block)
        view = wbuf.at[w_rows(block)]
        for j in range(1, near):
            send(view, view, wsem.at[block],
                 (g, (z * near + flip(y, j)) * 2 + c))
        cross(block)
        if k > 1:
            second(k - 1)
    second(deep - 1)

    total_rows = tokens + wide
    tiles = 4
    tile = total_rows // tiles

    def multiply(chip, first):
        at = pl.ds(aligned(chip * 2 * rows, 2 * rows), 2 * rows)

        @pl.loop(0, tiles)
        def _(i):
            here = pl.ds(aligned(i * tile, tile), tile)
            value = jnp.dot(st[here, at], wbuf[at, :], preferred_element_type=jnp.float32)
            if first:
                acc[here, :] = value
            else:
                acc[here, :] += value

    loads[2].wait()
    loads[4].wait()
    loads[5].wait()
    other_rows = st.at[pl.ds(aligned((1 - c) * tokens_here, tokens_here), tokens_here)]
    pltpu.make_async_copy(other_rows, other_rows, st_sem).wait()
    for h in range(own_parts):
        w_wait(p * groups + (1 - c) * own_parts + h)
    multiply(p, True)
    for j in range(1, near):
        chip = z * near + flip(y, j)
        for h in range(groups):
            w_wait(chip * groups + h)
        multiply(chip, False)
    for k in range(1, deep):
        for j in range(near):
            chip = flip(z, k) * near + flip(y, j)
            for h in range(1, groups):
                w_wait(chip * groups + lax.rem(g + h, groups))
            multiply(chip, False)

    for j in range(2):
        key = acc[:, j * HEAD_DIM : (j + 1) * HEAD_DIM]
        kb[j] = turn(key, cosine[...], sine[...]).astype(jnp.bfloat16)
        vb[j] = acc[:, HALF + j * HEAD_DIM : HALF + (j + 1) * HEAD_DIM].astype(jnp.bfloat16)
    nk[0] = kb[kv_slot, pl.ds(tokens, wide), :]
    nk[1] = vb[kv_slot, pl.ds(tokens, wide), :]
    send(nk, nkr, nsem, (g, mate))

    scale = HEAD_DIM ** (-0.5)
    for t in range(half):
        pltpu.make_async_copy(qbuf.at[t], qbuf.at[t], qsem.at[t]).wait()
    lanes = heads * wide
    pair = 2
    for t in range(0, half, pair):
        j = t // (half // 2)
        query = qbuf[pl.ds(t, pair)].reshape(pair * lanes, HEAD_DIM)
        scores = lax.dot_general(
            kb[j, pl.ds(0, tokens), :], query, (((1,), (1,)), ((), ())),
            preferred_element_type=jnp.float32,
        ) * scale
        if masked:
            prompt_row = jnp.concatenate([query_prompt[...]] * pair, axis=1)
            allowed = token_prompt[...] == prompt_row
            scores = jnp.where(allowed, scores, LOW)
        top = jnp.max(scores, axis=0, keepdims=True)
        weights = jnp.exp(scores - top)
        if masked:
            weights = jnp.where(allowed, weights, 0.0)
        total = jnp.sum(weights, axis=0, keepdims=True)
        value = lax.dot_general(
            vb[j, pl.ds(0, tokens), :], weights.astype(jnp.bfloat16), (((0,), (0,)), ((), ())),
            preferred_element_type=jnp.float32,
        )
        if masked:
            total = jnp.maximum(total, 1e-30)
        value = value / total
        mass = top + jnp.log(total)
        high = mass.astype(jnp.bfloat16).astype(jnp.float32)
        rest = mass - high
        middle = rest.astype(jnp.bfloat16).astype(jnp.float32)
        low = rest - middle
        row = lax.broadcasted_iota(jnp.int32, (TAIL, pair * lanes), 0)
        tail = jnp.where(row == 0, high, jnp.where(row == 1, middle, low))
        for u in range(pair):
            at = slice(u * lanes, (u + 1) * lanes)
            pout[t + u, pl.ds(0, HEAD_DIM), :] = value[:, at].astype(jnp.bfloat16)
            pout[t + u, pl.ds(HEAD_DIM, TAIL), :] = tail[:, at].astype(jnp.bfloat16)
        for u in range(pair):
            give(pout.at[t + u], pbuf.at[p], psem.at[p], c * half + t + u)

    pltpu.make_async_copy(nkr, nkr, nsem).wait()
    mine = kv_core == c
    new_key = jnp.where(mine, nk[0].astype(jnp.float32), nkr[0].astype(jnp.float32))
    new_value = jnp.where(mine, nk[1].astype(jnp.float32), nkr[1].astype(jnp.float32))

    def spread(value):
        return jnp.concatenate([value] * heads, axis=0)

    def earlier(value):
        return spread(jnp.concatenate([value[:samples], value[:samples]], axis=0))

    wide_query = qown[...].astype(jnp.float32)
    own = jnp.sum((wide_query * spread(new_key)).T, axis=0, keepdims=True) * scale
    back = jnp.sum((wide_query * earlier(new_key)).T, axis=0, keepdims=True) * scale
    lane = lax.broadcasted_iota(jnp.int32, (1, lanes), 1)
    late = lax.rem(lane, wide) >= samples
    back = jnp.where(late, back, LOW)
    high = jnp.maximum(own, back)
    masses = []
    for s in range(chips):
        pltpu.make_async_copy(pbuf.at[s], pbuf.at[s], psem.at[s]).wait()
    for s in range(chips):
        tail = pbuf[s, pl.ds(HEAD_DIM, TAIL), :].astype(jnp.float32)
        masses.append(tail[0:1] + tail[1:2] + tail[2:3])
        high = jnp.maximum(high, masses[-1])
    own = jnp.exp(own - high)
    back = jnp.where(late, jnp.exp(back - high), 0.0)
    below = own + back
    above = own * spread(new_value).T + back * earlier(new_value).T
    for s in range(chips):
        weight = jnp.exp(masses[s] - high)
        below += weight
        above += weight * pbuf[s, pl.ds(0, HEAD_DIM), :].astype(jnp.float32)
    head_out = (above / below).T
    flat = jnp.concatenate(
        [head_out[h * wide : (h + 1) * wide] for h in range(heads)], axis=1
    ).astype(jnp.bfloat16)

    loads[3].wait()

    def term(target):
        at = pl.ds(aligned(target * cols, cols), cols)
        return jnp.dot(flat, wob[:, at], preferred_element_type=jnp.float32)

    for k in reversed(range(chips)):
        chip = flip(p, k)
        tbuf[chip] = term(chip * 2 + 1 - c).astype(jnp.bfloat16)
        send(tbuf.at[chip], prbuf.at[chip], pair_sem.at[chip], (g, mate))
    for k in reversed(range(chips)):
        chip = flip(p, k)
        value = term(chip * 2 + c)
        pltpu.make_async_copy(prbuf.at[chip], prbuf.at[chip], pair_sem.at[chip]).wait()
        value = value + prbuf[chip].astype(jnp.float32)
        if k:
            sbuf[chip] = value.astype(jnp.bfloat16)
            send(sbuf.at[chip], rbuf.at[p], rsem.at[p], (g, chip * 2 + c))
        else:
            result = value
    for k in range(1, chips):
        chip = flip(p, k)
        pltpu.make_async_copy(rbuf.at[chip], rbuf.at[chip], rsem.at[chip]).wait()
        result = result + rbuf[chip].astype(jnp.float32)
    out[...] = result.astype(jnp.bfloat16)
    assert len(sends) == send_sem.shape[0]
    for copy, when in sends:
        if when is None:
            copy.wait_send()
        else:
            pl.when(when)(copy.wait_send)


def on_device(
    near,
    prompt_states,
    page_table,
    step_states,
    sample_order,
    key_weight,
    value_weight,
    query_weight,
    out_weight,
):
    groups = lax.axis_size("groups")
    devices = lax.axis_size("sample")
    chips = devices // 2
    own_chip = lax.axis_index("sample") // 2
    dim = prompt_states.shape[1]
    tokens = 2 * prompt_states.shape[0]
    chip_pages = tokens // PAGE
    heads = query_weight.shape[1] // HEAD_DIM
    total_pages = page_table.shape[0]
    prompts = total_pages // PROMPT_PAGES
    samples = sample_order.shape[0]
    wide = 2 * samples
    cols = dim // devices
    half = devices // 2
    lanes = heads * wide

    page_ids = own_chip * chip_pages + jnp.arange(chip_pages, dtype=jnp.int32)
    slots = jnp.sum(
        jnp.where(
            page_table[None, :] == page_ids[:, None],
            jnp.arange(total_pages, dtype=jnp.int32)[None, :],
            0,
        ),
        axis=1,
    )
    place = (slots % PROMPT_PAGES * PAGE)[:, None] + jnp.arange(PAGE, dtype=jnp.int32)[None, :]
    later = PROMPT_PAGES * PAGE + jnp.repeat(jnp.arange(2, dtype=jnp.int32), samples)
    position = jnp.concatenate([place.reshape(tokens), later]).astype(jnp.float32)
    lane = jnp.arange(HEAD_DIM, dtype=jnp.int32)
    order = (lane % (HEAD_DIM // 2)).astype(jnp.float32)
    frequency = ROPE_BASE ** (-order * 2.0 / HEAD_DIM)
    angle = position[:, None] * frequency[None, :]
    cosine = jnp.cos(angle)
    sine = jnp.where(lane < HEAD_DIM // 2, -1.0, 1.0)[None, :] * jnp.sin(angle)

    deep = chips // near
    send_count = (
        4 * (deep - 1)
        + groups // 2 * (4 * (near - 1) + 2)
        + (deep - 1) * (near - 1 + near * (groups - 1))
        + 3 * chips
        + half
        + 1
    )
    masked = prompts > 1
    args = [
        prompt_states,
        step_states.reshape(wide, dim),
        key_weight,
        value_weight,
        query_weight,
        out_weight,
        cosine,
        sine,
    ]
    specs = [pl.BlockSpec(memory_space=pl.ANY)] * 6 + [pl.BlockSpec(memory_space=pltpu.VMEM)] * 2
    if masked:
        token_prompt = jnp.repeat(slots // PROMPT_PAGES, PAGE)[:, None]
        query_prompt = jnp.tile(sample_order // (samples // prompts), 2 * heads)[None, :]
        args += [token_prompt, query_prompt]
        specs += [pl.BlockSpec(memory_space=pltpu.VMEM)] * 2
    bf16, f32 = jnp.bfloat16, jnp.float32
    dma = pltpu.SemaphoreType.DMA
    result = pl.pallas_call(
        functools.partial(kernel, (groups, devices, near, samples, heads, masked)),
        out_shape=jax.ShapeDtypeStruct((wide, cols), bf16),
        in_specs=specs,
        out_specs=pl.BlockSpec(memory_space=pltpu.VMEM),
        scratch_shapes=[
            pltpu.VMEM((tokens + wide, dim), bf16),
            pltpu.VMEM((dim, 2 * HALF), bf16),
            pltpu.VMEM((dim, heads * HEAD_DIM), bf16),
            pltpu.VMEM((heads * HEAD_DIM, dim), bf16),
            pltpu.VMEM((tokens + wide, 2 * HALF), f32),
            pltpu.VMEM((2, tokens + wide, HEAD_DIM), bf16),
            pltpu.VMEM((2, tokens + wide, HEAD_DIM), bf16),
            pltpu.VMEM((lanes, HEAD_DIM), bf16),
            pltpu.VMEM((half, lanes, HEAD_DIM), bf16),
            pltpu.VMEM((half, HEAD_DIM + TAIL, lanes), bf16),
            pltpu.VMEM((chips, HEAD_DIM + TAIL, lanes), bf16),
            pltpu.VMEM((2, wide, HEAD_DIM), bf16),
            pltpu.VMEM((2, wide, HEAD_DIM), bf16),
            pltpu.VMEM((chips, wide, cols), bf16),
            pltpu.VMEM((chips, wide, cols), bf16),
            pltpu.VMEM((chips, wide, cols), bf16),
            pltpu.VMEM((chips, wide, cols), bf16),
            dma((6,)),
            dma((send_count,)),
            dma((chips * groups,)),
            dma,
            dma((half,)),
            dma((chips,)),
            dma,
            dma((chips,)),
            dma((chips,)),
        ],
        compiler_params=pltpu.CompilerParams(
            collective_id=0, has_side_effects=True, vmem_limit_bytes=60 * 1024 * 1024
        ),
        name="prefill_decode",
    )(*args)
    return result.reshape(2, samples, cols)


def solution(mesh):
    in_specs = (
        P(("groups", "sample"), None),
        P("groups"),
        P(None, "groups", None),
        P("groups"),
        P("sample", None),
        P("sample", None),
        P(None, "sample"),
        P("sample", None),
    )
    out_specs = P(None, "groups", "sample")
    near = 2 if mesh.shape["groups"] == 2 else 1
    return jax.shard_map(
        functools.partial(on_device, near), mesh=mesh, in_specs=in_specs, out_specs=out_specs,
        check_vma=False,
    )
```

```python
import functools

import jax
import jax.numpy as jnp
import numpy as np
from jax import lax
from jax.experimental import pallas as pl
from jax.experimental.pallas import tpu as pltpu
from jax.sharding import PartitionSpec as P

HEAD_DIM = 128
KV_HEADS = 4
GQA = 8
PAGE = 128
PROMPT_PAGES = 64
HALF = KV_HEADS // 2 * HEAD_DIM
LOW = -1e30
TAIL = 16
CHUNKS = 2
MESH = pl.DeviceIdType.MESH
ROPE_BASE = 1000000.0


def flip(value, bits):
    result, weight = value, 1
    while weight <= bits:
        if bits & weight:
            result = result + weight * (1 - 2 * lax.rem(lax.div(value, weight), 2))
        weight *= 2
    return result


def turn(value, cosine, sine):
    return value * cosine + pltpu.roll(value, HEAD_DIM // 2, 1) * sine


def kernel(cfg, *refs):
    groups, devices, near, samples, heads, masked = cfg
    (states, step, wk, wv, wq, wo, page_table, frequency) = refs[:8]
    refs = refs[8:]
    if masked:
        token_prompt, query_prompt = refs[:2]
        refs = refs[2:]
    (out, cosine, sine, st, wbuf, wqb, wob, acc, kb, vb, qown, qbuf, pout, pbuf, nk, nkr, tbuf, prbuf, sbuf, rbuf,
     load_sem, send_sem, wsem, st_sem, qsem, psem, nsem, pair_sem, rsem) = refs
    chips = devices // 2
    deep = chips // near
    rows = wk.shape[0]
    part = 2 * rows // groups
    piece = part // CHUNKS
    own_parts = groups // 2
    tokens_here = states.shape[0]
    tokens = 2 * tokens_here
    wide = step.shape[0]
    dim = step.shape[1]
    cols = dim // devices
    half = devices // 2

    g = lax.axis_index("groups")
    me = lax.axis_index("sample")
    c = lax.rem(me, 2)
    p = lax.div(me, 2)
    y = lax.rem(p, near)
    z = lax.div(p, near)
    mate = p * 2 + 1 - c
    kv = lax.div(me * heads, GQA)
    kv_core = lax.div(kv, 2)
    kv_slot = lax.rem(kv, 2)

    def aligned(value, step_size):
        return pl.multiple_of(value, step_size)

    my_rows = pl.ds(aligned(c * tokens_here, tokens_here), tokens_here)
    loads = [
        pltpu.make_async_copy(step, st.at[pl.ds(tokens, wide)], load_sem.at[0]),
        pltpu.make_async_copy(wq, wqb, load_sem.at[1]),
        pltpu.make_async_copy(states, st.at[my_rows], load_sem.at[2]),
        pltpu.make_async_copy(wo, wob, load_sem.at[3]),
    ]
    own_w = pl.ds(aligned(me * rows, rows), rows)
    own_cols = pl.ds(aligned(c * HALF, HALF), HALF)
    loads.append(
        pltpu.make_async_copy(wk.at[:, own_cols], wbuf.at[own_w, pl.ds(0, HALF)], load_sem.at[4])
    )
    loads.append(
        pltpu.make_async_copy(wv.at[:, own_cols], wbuf.at[own_w, pl.ds(HALF, HALF)], load_sem.at[5])
    )
    for load in loads:
        load.start()

    barrier = pltpu.get_barrier_semaphore()
    for k in range(1, devices):
        pl.semaphore_signal(
            barrier, inc=1, device_id=(g, flip(me, k)), device_id_type=MESH
        )
    for k in range(1, groups):
        pl.semaphore_signal(
            barrier, inc=1, device_id=(lax.rem(g + k, groups), me), device_id_type=MESH
        )
    pl.semaphore_wait(barrier, devices + groups - 2)

    sends = []

    def send(src, dst, sem, target, when=None):
        copy = pltpu.make_async_remote_copy(
            src_ref=src, dst_ref=dst, send_sem=send_sem.at[len(sends)], recv_sem=sem,
            device_id=target, device_id_type=MESH,
        )
        if when is None:
            copy.start()
        else:
            pl.when(when)(copy.start)
        sends.append((copy, when))

    def block_of(chip, which, chunk):
        return (chip * groups + which) * CHUNKS + chunk

    def w_rows(block):
        return pl.ds(aligned(block * piece, piece), piece)

    def send_own(src_row, block, core, target, when=None):
        src_rows = pl.ds(src_row, piece)
        src_cols = pl.ds(aligned(core * HALF, HALF), HALF)
        send(wk.at[src_rows, src_cols], wbuf.at[w_rows(block), pl.ds(0, HALF)],
             wsem.at[block], target, when)
        send(wv.at[src_rows, src_cols], wbuf.at[w_rows(block), pl.ds(HALF, HALF)],
             wsem.at[block], target, when)

    def w_wait(block):
        view = wbuf.at[w_rows(block)]
        pltpu.make_async_copy(view, view, wsem.at[block]).wait()

    def along(shift):
        return lax.rem(z + shift + deep, deep)

    def inside(shift):
        return jnp.logical_and(z + shift >= 0, z + shift < deep)

    def to_line(h, when):
        which = c * own_parts + h
        for chunk in range(CHUNKS):
            for shift in (1, -1):
                go = jnp.logical_and(when(which), inside(shift))
                for core in range(2):
                    target = (g, (along(shift) * near + y) * 2 + core)
                    send_own(h * part + chunk * piece, block_of(p, which, chunk), core, target, go)

    def to_near(chunk):
        for h in range(own_parts):
            for k in range(1, near):
                chip = z * near + flip(y, k)
                for core in range(2):
                    send_own(h * part + chunk * piece, block_of(p, c * own_parts + h, chunk), core,
                             (g, chip * 2 + core))

    for h in range(own_parts):
        to_line(h, lambda which: which == g)
    to_near(0)
    for h in range(own_parts):
        for chunk in range(CHUNKS):
            send_own(h * part + chunk * piece, block_of(p, c * own_parts + h, chunk), 1 - c,
                     (g, mate))
    send(states, st.at[my_rows], st_sem, (g, mate))

    loads[0].wait()
    loads[1].wait()
    depth = 1024

    def q_step(i, total):
        at = pl.ds(aligned(i * depth, depth), depth)
        return total + jnp.dot(
            st[pl.ds(tokens, wide), at], wqb[at, :], preferred_element_type=jnp.float32
        )

    queries = lax.fori_loop(
        0, dim // depth, q_step, jnp.zeros((wide, heads * HEAD_DIM), jnp.float32)
    )
    lane_row = lax.broadcasted_iota(jnp.int32, (1, HEAD_DIM), 1)
    sign = jnp.where(lane_row < HEAD_DIM // 2, -1.0, 1.0)
    rate = frequency[...]
    late_row = lax.broadcasted_iota(jnp.int32, (wide, HEAD_DIM), 0) >= samples
    step_angle = (PROMPT_PAGES * PAGE + jnp.where(late_row, 1.0, 0.0)) * rate
    cosine[pl.ds(tokens, wide), :] = jnp.cos(step_angle)
    sine[pl.ds(tokens, wide), :] = jnp.sin(step_angle) * sign
    step_cos = cosine[pl.ds(tokens, wide), :]
    step_sin = sine[pl.ds(tokens, wide), :]
    for h in range(heads):
        one = queries[:, h * HEAD_DIM : (h + 1) * HEAD_DIM]
        qown[pl.ds(h * wide, wide), :] = turn(one, step_cos, step_sin).astype(jnp.bfloat16)

    def give(src, dst, sem, target):
        send(src, dst, sem, (g, target), target != me)

        @pl.when(target == me)
        def _():
            pltpu.make_async_copy(src, dst, sem).start()

    q_slot = lax.rem(me, half)
    for k in range(chips):
        give(qown, qbuf.at[q_slot], qsem.at[q_slot], flip(p, k) * 2 + kv_core)

    def cross(block, when):
        view = wbuf.at[w_rows(block)]
        for k in range(1, groups):
            send(view, view, wsem.at[block], (lax.rem(g + k, groups), me), when)

    def line(d):
        for chunk in range(CHUNKS):
            for shift in (d, -d):
                here = inside(shift)
                block = block_of(along(shift) * near + y, g, chunk)
                pl.when(here)(functools.partial(w_wait, block))
                view = wbuf.at[w_rows(block)]
                on = -1 if shift > 0 else 1
                for j in range(1, near):
                    send(view, view, wsem.at[block], (g, (z * near + flip(y, j)) * 2 + c), here)
                if d < deep - 1:
                    send(view, view, wsem.at[block], (g, (along(on) * near + y) * 2 + c),
                         jnp.logical_and(here, inside(on)))
                if d > 1:
                    cross(block, here)

    def second(d):
        for j in range(1, near):
            for chunk in range(CHUNKS):
                for shift in (d, -d):
                    here = inside(shift)
                    block = block_of(along(shift) * near + flip(y, j), g, chunk)
                    pl.when(here)(functools.partial(w_wait, block))
                    cross(block, here)

    line(1)
    for h in range(own_parts):
        to_line(h, lambda which: which != g)
    for chunk in range(1, CHUNKS):
        to_near(chunk)
    for d in range(2, deep):
        line(d)
        second(d - 1)
    second(deep - 1)

    page_row = lax.broadcasted_iota(jnp.int32, (tokens // PAGE, page_table.shape[1]), 0)
    entry = lax.broadcasted_iota(jnp.int32, (tokens // PAGE, page_table.shape[1]), 1)
    match = page_table[...] == page_row + p * (tokens // PAGE)
    slot = jnp.sum(
        jnp.where(match, lax.rem(entry, PROMPT_PAGES).astype(jnp.float32), 0.0),
        axis=1, keepdims=True,
    )
    base_angle = slot * float(PAGE) * rate
    base_cos, base_sin = jnp.cos(base_angle), jnp.sin(base_angle)
    row_angle = lax.broadcasted_iota(jnp.int32, (PAGE, HEAD_DIM), 0).astype(jnp.float32) * rate
    row_cos, row_sin = jnp.cos(row_angle), jnp.sin(row_angle)
    for i in range(tokens // PAGE):
        one_cos, one_sin = base_cos[i : i + 1], base_sin[i : i + 1]
        cosine[pl.ds(i * PAGE, PAGE), :] = one_cos * row_cos - one_sin * row_sin
        sine[pl.ds(i * PAGE, PAGE), :] = (one_sin * row_cos + one_cos * row_sin) * sign

    total_rows = tokens + wide
    tiles = 4
    tile = total_rows // tiles

    def multiply(chip, first):
        at = pl.ds(aligned(chip * 2 * rows, 2 * rows), 2 * rows)

        @pl.loop(0, tiles)
        def _(i):
            here = pl.ds(aligned(i * tile, tile), tile)
            value = jnp.dot(st[here, at], wbuf[at, :], preferred_element_type=jnp.float32)
            if first:
                acc[here, :] = value
            else:
                acc[here, :] += value

    loads[2].wait()
    loads[4].wait()
    loads[5].wait()
    other_rows = st.at[pl.ds(aligned((1 - c) * tokens_here, tokens_here), tokens_here)]
    pltpu.make_async_copy(other_rows, other_rows, st_sem).wait()
    for h in range(own_parts):
        for chunk in range(CHUNKS):
            w_wait(block_of(p, (1 - c) * own_parts + h, chunk))
    multiply(p, True)
    for j in range(1, near):
        chip = z * near + flip(y, j)
        for h in range(groups):
            for chunk in range(CHUNKS):
                w_wait(block_of(chip, h, chunk))
        multiply(chip, False)
    for j in range(near):
        for k in range(1, deep):
            chip = flip(z, k) * near + flip(y, j)
            for h in range(1, groups):
                for chunk in range(CHUNKS):
                    w_wait(block_of(chip, lax.rem(g + h, groups), chunk))
            multiply(chip, False)

    for j in range(2):
        key = acc[:, j * HEAD_DIM : (j + 1) * HEAD_DIM]
        kb[j] = turn(key, cosine[...], sine[...]).astype(jnp.bfloat16)
        vb[j] = acc[:, HALF + j * HEAD_DIM : HALF + (j + 1) * HEAD_DIM].astype(jnp.bfloat16)
    nk[0] = kb[kv_slot, pl.ds(tokens, wide), :]
    nk[1] = vb[kv_slot, pl.ds(tokens, wide), :]
    send(nk, nkr, nsem, (g, mate))

    scale = HEAD_DIM ** (-0.5)
    for t in range(half):
        pltpu.make_async_copy(qbuf.at[t], qbuf.at[t], qsem.at[t]).wait()
    lanes = heads * wide
    pair = 2
    for t in range(0, half, pair):
        j = t // (half // 2)
        query = qbuf[pl.ds(t, pair)].reshape(pair * lanes, HEAD_DIM)
        scores = lax.dot_general(
            kb[j, pl.ds(0, tokens), :], query, (((1,), (1,)), ((), ())),
            preferred_element_type=jnp.float32,
        ) * scale
        if masked:
            prompt_row = jnp.concatenate([query_prompt[...]] * pair, axis=1)
            allowed = token_prompt[...] == prompt_row
            scores = jnp.where(allowed, scores, LOW)
        top = jnp.max(scores, axis=0, keepdims=True)
        weights = jnp.exp(scores - top)
        if masked:
            weights = jnp.where(allowed, weights, 0.0)
        total = jnp.sum(weights, axis=0, keepdims=True)
        value = lax.dot_general(
            vb[j, pl.ds(0, tokens), :], weights.astype(jnp.bfloat16), (((0,), (0,)), ((), ())),
            preferred_element_type=jnp.float32,
        )
        if masked:
            total = jnp.maximum(total, 1e-30)
        value = value / total
        mass = top + jnp.log(total)
        high = mass.astype(jnp.bfloat16).astype(jnp.float32)
        rest = mass - high
        middle = rest.astype(jnp.bfloat16).astype(jnp.float32)
        low = rest - middle
        row = lax.broadcasted_iota(jnp.int32, (TAIL, pair * lanes), 0)
        tail = jnp.where(row == 0, high, jnp.where(row == 1, middle, low))
        for u in range(pair):
            at = slice(u * lanes, (u + 1) * lanes)
            pout[t + u, pl.ds(0, HEAD_DIM), :] = value[:, at].astype(jnp.bfloat16)
            pout[t + u, pl.ds(HEAD_DIM, TAIL), :] = tail[:, at].astype(jnp.bfloat16)
        for u in range(pair):
            give(pout.at[t + u], pbuf.at[p], psem.at[p], c * half + t + u)

    pltpu.make_async_copy(nkr, nkr, nsem).wait()
    mine = kv_core == c
    new_key = jnp.where(mine, nk[0].astype(jnp.float32), nkr[0].astype(jnp.float32))
    new_value = jnp.where(mine, nk[1].astype(jnp.float32), nkr[1].astype(jnp.float32))

    def spread(value):
        return jnp.concatenate([value] * heads, axis=0)

    def earlier(value):
        return spread(jnp.concatenate([value[:samples], value[:samples]], axis=0))

    wide_query = qown[...].astype(jnp.float32)
    own = jnp.sum((wide_query * spread(new_key)).T, axis=0, keepdims=True) * scale
    back = jnp.sum((wide_query * earlier(new_key)).T, axis=0, keepdims=True) * scale
    lane = lax.broadcasted_iota(jnp.int32, (1, lanes), 1)
    late = lax.rem(lane, wide) >= samples
    back = jnp.where(late, back, LOW)
    high = jnp.maximum(own, back)
    masses = []
    for s in range(chips):
        pltpu.make_async_copy(pbuf.at[s], pbuf.at[s], psem.at[s]).wait()
    for s in range(chips):
        tail = pbuf[s, pl.ds(HEAD_DIM, TAIL), :].astype(jnp.float32)
        masses.append(tail[0:1] + tail[1:2] + tail[2:3])
        high = jnp.maximum(high, masses[-1])
    own = jnp.exp(own - high)
    back = jnp.where(late, jnp.exp(back - high), 0.0)
    below = own + back
    above = own * spread(new_value).T + back * earlier(new_value).T
    for s in range(chips):
        weight = jnp.exp(masses[s] - high)
        below += weight
        above += weight * pbuf[s, pl.ds(0, HEAD_DIM), :].astype(jnp.float32)
    head_out = (above / below).T
    flat = jnp.concatenate(
        [head_out[h * wide : (h + 1) * wide] for h in range(heads)], axis=1
    ).astype(jnp.bfloat16)

    loads[3].wait()

    def term(target):
        at = pl.ds(aligned(target * cols, cols), cols)
        return jnp.dot(flat, wob[:, at], preferred_element_type=jnp.float32)

    for k in reversed(range(chips)):
        chip = flip(p, k)
        tbuf[chip] = term(chip * 2 + 1 - c).astype(jnp.bfloat16)
        send(tbuf.at[chip], prbuf.at[chip], pair_sem.at[chip], (g, mate))
    for k in reversed(range(chips)):
        chip = flip(p, k)
        value = term(chip * 2 + c)
        pltpu.make_async_copy(prbuf.at[chip], prbuf.at[chip], pair_sem.at[chip]).wait()
        value = value + prbuf[chip].astype(jnp.float32)
        if k:
            sbuf[chip] = value.astype(jnp.bfloat16)
            send(sbuf.at[chip], rbuf.at[p], rsem.at[p], (g, chip * 2 + c))
        else:
            result = value
    for k in range(1, chips):
        chip = flip(p, k)
        pltpu.make_async_copy(rbuf.at[chip], rbuf.at[chip], rsem.at[chip]).wait()
        result = result + rbuf[chip].astype(jnp.float32)
    out[...] = result.astype(jnp.bfloat16)
    assert len(sends) == send_sem.shape[0]
    for copy, when in sends:
        if when is None:
            copy.wait_send()
        else:
            pl.when(when)(copy.wait_send)


def on_device(
    near,
    prompt_states,
    page_table,
    step_states,
    sample_order,
    key_weight,
    value_weight,
    query_weight,
    out_weight,
):
    groups = lax.axis_size("groups")
    devices = lax.axis_size("sample")
    chips = devices // 2
    own_chip = lax.axis_index("sample") // 2
    dim = prompt_states.shape[1]
    tokens = 2 * prompt_states.shape[0]
    chip_pages = tokens // PAGE
    heads = query_weight.shape[1] // HEAD_DIM
    total_pages = page_table.shape[0]
    prompts = total_pages // PROMPT_PAGES
    samples = sample_order.shape[0]
    wide = 2 * samples
    cols = dim // devices
    half = devices // 2
    lanes = heads * wide

    order = np.arange(HEAD_DIM) % (HEAD_DIM // 2)
    frequency = jnp.asarray((ROPE_BASE ** (-order * 2.0 / HEAD_DIM)).astype(np.float32))[None, :]
    deep = chips // near
    own_parts = groups // 2
    send_count = (
        CHUNKS * own_parts * (16 + 2 + 4 * (near - 1))
        + 2 * CHUNKS * (deep - 1) * near
        + 2 * CHUNKS * (deep - 2) * groups
        - 2 * CHUNKS * (deep - 2) * 1
        + 2 * CHUNKS * (deep - 1) * (near - 1) * (groups - 1)
        - 2 * CHUNKS * (deep - 1)
        + 2 * CHUNKS * (deep - 2)
        + 3 * chips
        + half
        + 1
    )
    masked = prompts > 1
    args = [
        prompt_states,
        step_states.reshape(wide, dim),
        key_weight,
        value_weight,
        query_weight,
        out_weight,
        page_table[None, :],
        frequency,
    ]
    specs = [pl.BlockSpec(memory_space=pl.ANY)] * 6 + [pl.BlockSpec(memory_space=pltpu.VMEM)] * 2
    if masked:
        page_ids = own_chip * chip_pages + jnp.arange(chip_pages, dtype=jnp.int32)
        slots = jnp.sum(
            jnp.where(
                page_table[None, :] == page_ids[:, None],
                jnp.arange(total_pages, dtype=jnp.int32)[None, :],
                0,
            ),
            axis=1,
        )
        token_prompt = jnp.repeat(slots // PROMPT_PAGES, PAGE)[:, None]
        query_prompt = jnp.tile(sample_order // (samples // prompts), 2 * heads)[None, :]
        args += [token_prompt, query_prompt]
        specs += [pl.BlockSpec(memory_space=pltpu.VMEM)] * 2
    bf16, f32 = jnp.bfloat16, jnp.float32
    dma = pltpu.SemaphoreType.DMA
    result = pl.pallas_call(
        functools.partial(kernel, (groups, devices, near, samples, heads, masked)),
        out_shape=jax.ShapeDtypeStruct((wide, cols), bf16),
        in_specs=specs,
        out_specs=pl.BlockSpec(memory_space=pltpu.VMEM),
        scratch_shapes=[
            pltpu.VMEM((tokens + wide, HEAD_DIM), f32),
            pltpu.VMEM((tokens + wide, HEAD_DIM), f32),
            pltpu.VMEM((tokens + wide, dim), bf16),
            pltpu.VMEM((dim, 2 * HALF), bf16),
            pltpu.VMEM((dim, heads * HEAD_DIM), bf16),
            pltpu.VMEM((heads * HEAD_DIM, dim), bf16),
            pltpu.VMEM((tokens + wide, 2 * HALF), f32),
            pltpu.VMEM((2, tokens + wide, HEAD_DIM), bf16),
            pltpu.VMEM((2, tokens + wide, HEAD_DIM), bf16),
            pltpu.VMEM((lanes, HEAD_DIM), bf16),
            pltpu.VMEM((half, lanes, HEAD_DIM), bf16),
            pltpu.VMEM((half, HEAD_DIM + TAIL, lanes), bf16),
            pltpu.VMEM((chips, HEAD_DIM + TAIL, lanes), bf16),
            pltpu.VMEM((2, wide, HEAD_DIM), bf16),
            pltpu.VMEM((2, wide, HEAD_DIM), bf16),
            pltpu.VMEM((chips, wide, cols), bf16),
            pltpu.VMEM((chips, wide, cols), bf16),
            pltpu.VMEM((chips, wide, cols), bf16),
            pltpu.VMEM((chips, wide, cols), bf16),
            dma((6,)),
            dma((send_count,)),
            dma((chips * groups * CHUNKS,)),
            dma,
            dma((half,)),
            dma((chips,)),
            dma,
            dma((chips,)),
            dma((chips,)),
        ],
        compiler_params=pltpu.CompilerParams(
            collective_id=0, has_side_effects=True, vmem_limit_bytes=60 * 1024 * 1024
        ),
        name="prefill_decode",
    )(*args)
    return result.reshape(2, samples, cols)


def solution(mesh):
    in_specs = (
        P(("groups", "sample"), None),
        P("groups"),
        P(None, "groups", None),
        P("groups"),
        P("sample", None),
        P("sample", None),
        P(None, "sample"),
        P("sample", None),
    )
    out_specs = P(None, "groups", "sample")
    near = 2 if mesh.shape["groups"] == 2 else 1
    return jax.shard_map(
        functools.partial(on_device, near), mesh=mesh, in_specs=in_specs, out_specs=out_specs,
        check_vma=False,
    )
```

```python
import functools

import jax
import jax.numpy as jnp
import numpy as np
from jax import lax
from jax.experimental import pallas as pl
from jax.experimental.pallas import tpu as pltpu
from jax.sharding import PartitionSpec as P

HEAD_DIM = 128
KV_HEADS = 4
GQA = 8
PAGE = 128
PROMPT_PAGES = 64
HALF = KV_HEADS // 2 * HEAD_DIM
LOW = -1e30
TAIL = 16
CHUNKS = 2
MESH = pl.DeviceIdType.MESH
ROPE_BASE = 1000000.0


def flip(value, bits):
    result, weight = value, 1
    while weight <= bits:
        if bits & weight:
            result = result + weight * (1 - 2 * lax.rem(lax.div(value, weight), 2))
        weight *= 2
    return result


def turn(value, cosine, sine):
    return value * cosine + pltpu.roll(value, HEAD_DIM // 2, 1) * sine


def kernel(cfg, *refs):
    groups, devices, near, samples, heads, masked = cfg
    (states, step, wk, wv, wq, wo, page_table, frequency) = refs[:8]
    refs = refs[8:]
    if masked:
        token_prompt, query_prompt = refs[:2]
        refs = refs[2:]
    (out, cosine, sine, st, wbuf, wqb, wob, acc, kb, vb, qown, qbuf, pout, pbuf, nk, nkr, tbuf, prbuf, sbuf, rbuf,
     load_sem, send_sem, wsem, st_sem, qsem, psem, nsem, pair_sem, rsem) = refs
    chips = devices // 2
    deep = chips // near
    rows = wk.shape[0]
    part = 2 * rows // groups
    piece = part // CHUNKS
    own_parts = groups // 2
    tokens_here = states.shape[0]
    tokens = 2 * tokens_here
    wide = step.shape[0]
    dim = step.shape[1]
    cols = dim // devices
    half = devices // 2

    g = lax.axis_index("groups")
    me = lax.axis_index("sample")
    c = lax.rem(me, 2)
    p = lax.div(me, 2)
    y = lax.rem(p, near)
    z = lax.div(p, near)
    mate = p * 2 + 1 - c
    kv = lax.div(me * heads, GQA)
    kv_core = lax.div(kv, 2)
    kv_slot = lax.rem(kv, 2)

    def aligned(value, step_size):
        return pl.multiple_of(value, step_size)

    my_rows = pl.ds(aligned(c * tokens_here, tokens_here), tokens_here)
    loads = [
        pltpu.make_async_copy(step, st.at[pl.ds(tokens, wide)], load_sem.at[0]),
        pltpu.make_async_copy(wq, wqb, load_sem.at[1]),
        pltpu.make_async_copy(states, st.at[my_rows], load_sem.at[2]),
        pltpu.make_async_copy(wo, wob, load_sem.at[3]),
    ]
    own_w = pl.ds(aligned(me * rows, rows), rows)
    own_cols = pl.ds(aligned(c * HALF, HALF), HALF)
    loads.append(
        pltpu.make_async_copy(wk.at[:, own_cols], wbuf.at[own_w, pl.ds(0, HALF)], load_sem.at[4])
    )
    loads.append(
        pltpu.make_async_copy(wv.at[:, own_cols], wbuf.at[own_w, pl.ds(HALF, HALF)], load_sem.at[5])
    )
    barrier = pltpu.get_barrier_semaphore()
    for k in range(1, devices):
        pl.semaphore_signal(
            barrier, inc=1, device_id=(g, flip(me, k)), device_id_type=MESH
        )
    for k in range(1, groups):
        pl.semaphore_signal(
            barrier, inc=1, device_id=(lax.rem(g + k, groups), me), device_id_type=MESH
        )
    pl.semaphore_wait(barrier, devices + groups - 2)

    sends = []

    def send(src, dst, sem, target, when=None):
        copy = pltpu.make_async_remote_copy(
            src_ref=src, dst_ref=dst, send_sem=send_sem.at[len(sends)], recv_sem=sem,
            device_id=target, device_id_type=MESH,
        )
        if when is None:
            copy.start()
        else:
            pl.when(when)(copy.start)
        sends.append((copy, when))

    def block_of(chip, which, chunk):
        return (chip * groups + which) * CHUNKS + chunk

    def w_rows(block):
        return pl.ds(aligned(block * piece, piece), piece)

    def send_own(src_row, block, core, target, when=None):
        src_rows = pl.ds(src_row, piece)
        src_cols = pl.ds(aligned(core * HALF, HALF), HALF)
        send(wk.at[src_rows, src_cols], wbuf.at[w_rows(block), pl.ds(0, HALF)],
             wsem.at[block], target, when)
        send(wv.at[src_rows, src_cols], wbuf.at[w_rows(block), pl.ds(HALF, HALF)],
             wsem.at[block], target, when)

    def w_wait(block):
        view = wbuf.at[w_rows(block)]
        pltpu.make_async_copy(view, view, wsem.at[block]).wait()

    def along(shift):
        return lax.rem(z + shift + deep, deep)

    def inside(shift):
        return jnp.logical_and(z + shift >= 0, z + shift < deep)

    def to_line(h, when):
        which = c * own_parts + h
        for chunk in range(CHUNKS):
            for shift in (1, -1):
                go = jnp.logical_and(when(which), inside(shift))
                for core in range(2):
                    target = (g, (along(shift) * near + y) * 2 + core)
                    send_own(h * part + chunk * piece, block_of(p, which, chunk), core, target, go)

    def to_near(chunk):
        for h in range(own_parts):
            for k in range(1, near):
                chip = z * near + flip(y, k)
                for core in range(2):
                    send_own(h * part + chunk * piece, block_of(p, c * own_parts + h, chunk), core,
                             (g, chip * 2 + core))

    for h in range(own_parts):
        to_line(h, lambda which: which == g)
    to_near(0)
    for h in range(own_parts):
        for chunk in range(CHUNKS):
            send_own(h * part + chunk * piece, block_of(p, c * own_parts + h, chunk), 1 - c,
                     (g, mate))
    send(states, st.at[my_rows], st_sem, (g, mate))
    for load in loads:
        load.start()

    def cross(block, when):
        view = wbuf.at[w_rows(block)]
        for k in range(1, groups):
            send(view, view, wsem.at[block], (lax.rem(g + k, groups), me), when)

    def line(d):
        for chunk in range(CHUNKS):
            for shift in (d, -d):
                here = inside(shift)
                block = block_of(along(shift) * near + y, g, chunk)
                pl.when(here)(functools.partial(w_wait, block))
                view = wbuf.at[w_rows(block)]
                on = -1 if shift > 0 else 1
                for j in range(1, near):
                    send(view, view, wsem.at[block], (g, (z * near + flip(y, j)) * 2 + c), here)
                if d < deep - 1:
                    send(view, view, wsem.at[block], (g, (along(on) * near + y) * 2 + c),
                         jnp.logical_and(here, inside(on)))
                if d > 1:
                    cross(block, here)

    def second(d):
        for j in range(1, near):
            for chunk in range(CHUNKS):
                for shift in (d, -d):
                    here = inside(shift)
                    block = block_of(along(shift) * near + flip(y, j), g, chunk)
                    pl.when(here)(functools.partial(w_wait, block))
                    cross(block, here)

    line(1)
    for h in range(own_parts):
        to_line(h, lambda which: which != g)
    for chunk in range(1, CHUNKS):
        to_near(chunk)
    for d in range(2, deep):
        line(d)
        second(d - 1)
    second(deep - 1)

    loads[0].wait()
    loads[1].wait()
    depth = 1024

    def q_step(i, total):
        at = pl.ds(aligned(i * depth, depth), depth)
        return total + jnp.dot(
            st[pl.ds(tokens, wide), at], wqb[at, :], preferred_element_type=jnp.float32
        )

    queries = lax.fori_loop(
        0, dim // depth, q_step, jnp.zeros((wide, heads * HEAD_DIM), jnp.float32)
    )
    lane_row = lax.broadcasted_iota(jnp.int32, (1, HEAD_DIM), 1)
    sign = jnp.where(lane_row < HEAD_DIM // 2, -1.0, 1.0)
    rate = frequency[...]
    late_row = lax.broadcasted_iota(jnp.int32, (wide, HEAD_DIM), 0) >= samples
    step_angle = (PROMPT_PAGES * PAGE + jnp.where(late_row, 1.0, 0.0)) * rate
    cosine[pl.ds(tokens, wide), :] = jnp.cos(step_angle)
    sine[pl.ds(tokens, wide), :] = jnp.sin(step_angle) * sign
    step_cos = cosine[pl.ds(tokens, wide), :]
    step_sin = sine[pl.ds(tokens, wide), :]
    for h in range(heads):
        one = queries[:, h * HEAD_DIM : (h + 1) * HEAD_DIM]
        qown[pl.ds(h * wide, wide), :] = turn(one, step_cos, step_sin).astype(jnp.bfloat16)

    def give(src, dst, sem, target):
        send(src, dst, sem, (g, target), target != me)

        @pl.when(target == me)
        def _():
            pltpu.make_async_copy(src, dst, sem).start()

    q_slot = lax.rem(me, half)
    for k in range(chips):
        give(qown, qbuf.at[q_slot], qsem.at[q_slot], flip(p, k) * 2 + kv_core)

    page_row = lax.broadcasted_iota(jnp.int32, (tokens // PAGE, page_table.shape[1]), 0)
    entry = lax.broadcasted_iota(jnp.int32, (tokens // PAGE, page_table.shape[1]), 1)
    match = page_table[...] == page_row + p * (tokens // PAGE)
    slot = jnp.sum(
        jnp.where(match, lax.rem(entry, PROMPT_PAGES).astype(jnp.float32), 0.0),
        axis=1, keepdims=True,
    )
    base_angle = slot * float(PAGE) * rate
    base_cos, base_sin = jnp.cos(base_angle), jnp.sin(base_angle)
    row_angle = lax.broadcasted_iota(jnp.int32, (PAGE, HEAD_DIM), 0).astype(jnp.float32) * rate
    row_cos, row_sin = jnp.cos(row_angle), jnp.sin(row_angle)
    for i in range(tokens // PAGE):
        one_cos, one_sin = base_cos[i : i + 1], base_sin[i : i + 1]
        cosine[pl.ds(i * PAGE, PAGE), :] = one_cos * row_cos - one_sin * row_sin
        sine[pl.ds(i * PAGE, PAGE), :] = (one_sin * row_cos + one_cos * row_sin) * sign

    total_rows = tokens + wide
    tiles = 4
    tile = total_rows // tiles

    def multiply(chip, first):
        at = pl.ds(aligned(chip * 2 * rows, 2 * rows), 2 * rows)

        @pl.loop(0, tiles)
        def _(i):
            here = pl.ds(aligned(i * tile, tile), tile)
            value = jnp.dot(st[here, at], wbuf[at, :], preferred_element_type=jnp.float32)
            if first:
                acc[here, :] = value
            else:
                acc[here, :] += value

    loads[2].wait()
    loads[4].wait()
    loads[5].wait()
    other_rows = st.at[pl.ds(aligned((1 - c) * tokens_here, tokens_here), tokens_here)]
    pltpu.make_async_copy(other_rows, other_rows, st_sem).wait()
    for h in range(own_parts):
        for chunk in range(CHUNKS):
            w_wait(block_of(p, (1 - c) * own_parts + h, chunk))
    multiply(p, True)
    for j in range(1, near):
        chip = z * near + flip(y, j)
        for h in range(groups):
            for chunk in range(CHUNKS):
                w_wait(block_of(chip, h, chunk))
        multiply(chip, False)
    for j in range(near):
        for k in range(1, deep):
            chip = flip(z, k) * near + flip(y, j)
            for h in range(1, groups):
                for chunk in range(CHUNKS):
                    w_wait(block_of(chip, lax.rem(g + h, groups), chunk))
            multiply(chip, False)

    for j in range(2):
        key = acc[:, j * HEAD_DIM : (j + 1) * HEAD_DIM]
        kb[j] = turn(key, cosine[...], sine[...]).astype(jnp.bfloat16)
        vb[j] = acc[:, HALF + j * HEAD_DIM : HALF + (j + 1) * HEAD_DIM].astype(jnp.bfloat16)
    nk[0] = kb[kv_slot, pl.ds(tokens, wide), :]
    nk[1] = vb[kv_slot, pl.ds(tokens, wide), :]
    send(nk, nkr, nsem, (g, mate))

    scale = HEAD_DIM ** (-0.5)
    for t in range(half):
        pltpu.make_async_copy(qbuf.at[t], qbuf.at[t], qsem.at[t]).wait()
    lanes = heads * wide
    pair = 2
    for t in range(0, half, pair):
        j = t // (half // 2)
        query = qbuf[pl.ds(t, pair)].reshape(pair * lanes, HEAD_DIM)
        scores = lax.dot_general(
            kb[j, pl.ds(0, tokens), :], query, (((1,), (1,)), ((), ())),
            preferred_element_type=jnp.float32,
        ) * scale
        if masked:
            prompt_row = jnp.concatenate([query_prompt[...]] * pair, axis=1)
            allowed = token_prompt[...] == prompt_row
            scores = jnp.where(allowed, scores, LOW)
        top = jnp.max(scores, axis=0, keepdims=True)
        weights = jnp.exp(scores - top)
        if masked:
            weights = jnp.where(allowed, weights, 0.0)
        total = jnp.sum(weights, axis=0, keepdims=True)
        value = lax.dot_general(
            vb[j, pl.ds(0, tokens), :], weights.astype(jnp.bfloat16), (((0,), (0,)), ((), ())),
            preferred_element_type=jnp.float32,
        )
        if masked:
            total = jnp.maximum(total, 1e-30)
        value = value / total
        mass = top + jnp.log(total)
        high = mass.astype(jnp.bfloat16).astype(jnp.float32)
        rest = mass - high
        middle = rest.astype(jnp.bfloat16).astype(jnp.float32)
        low = rest - middle
        row = lax.broadcasted_iota(jnp.int32, (TAIL, pair * lanes), 0)
        tail = jnp.where(row == 0, high, jnp.where(row == 1, middle, low))
        for u in range(pair):
            at = slice(u * lanes, (u + 1) * lanes)
            pout[t + u, pl.ds(0, HEAD_DIM), :] = value[:, at].astype(jnp.bfloat16)
            pout[t + u, pl.ds(HEAD_DIM, TAIL), :] = tail[:, at].astype(jnp.bfloat16)
        for u in range(pair):
            give(pout.at[t + u], pbuf.at[p], psem.at[p], c * half + t + u)

    pltpu.make_async_copy(nkr, nkr, nsem).wait()
    mine = kv_core == c
    new_key = jnp.where(mine, nk[0].astype(jnp.float32), nkr[0].astype(jnp.float32))
    new_value = jnp.where(mine, nk[1].astype(jnp.float32), nkr[1].astype(jnp.float32))

    def spread(value):
        return jnp.concatenate([value] * heads, axis=0)

    def earlier(value):
        return spread(jnp.concatenate([value[:samples], value[:samples]], axis=0))

    wide_query = qown[...].astype(jnp.float32)
    own = jnp.sum((wide_query * spread(new_key)).T, axis=0, keepdims=True) * scale
    back = jnp.sum((wide_query * earlier(new_key)).T, axis=0, keepdims=True) * scale
    lane = lax.broadcasted_iota(jnp.int32, (1, lanes), 1)
    late = lax.rem(lane, wide) >= samples
    back = jnp.where(late, back, LOW)
    high = jnp.maximum(own, back)
    masses = []
    for s in range(chips):
        pltpu.make_async_copy(pbuf.at[s], pbuf.at[s], psem.at[s]).wait()
    for s in range(chips):
        tail = pbuf[s, pl.ds(HEAD_DIM, TAIL), :].astype(jnp.float32)
        masses.append(tail[0:1] + tail[1:2] + tail[2:3])
        high = jnp.maximum(high, masses[-1])
    own = jnp.exp(own - high)
    back = jnp.where(late, jnp.exp(back - high), 0.0)
    below = own + back
    above = own * spread(new_value).T + back * earlier(new_value).T
    for s in range(chips):
        weight = jnp.exp(masses[s] - high)
        below += weight
        above += weight * pbuf[s, pl.ds(0, HEAD_DIM), :].astype(jnp.float32)
    head_out = (above / below).T
    flat = jnp.concatenate(
        [head_out[h * wide : (h + 1) * wide] for h in range(heads)], axis=1
    ).astype(jnp.bfloat16)

    loads[3].wait()

    def term(target):
        at = pl.ds(aligned(target * cols, cols), cols)
        return jnp.dot(flat, wob[:, at], preferred_element_type=jnp.float32)

    for k in reversed(range(chips)):
        chip = flip(p, k)
        tbuf[chip] = term(chip * 2 + 1 - c).astype(jnp.bfloat16)
        send(tbuf.at[chip], prbuf.at[chip], pair_sem.at[chip], (g, mate))
    for k in reversed(range(chips)):
        chip = flip(p, k)
        value = term(chip * 2 + c)
        pltpu.make_async_copy(prbuf.at[chip], prbuf.at[chip], pair_sem.at[chip]).wait()
        value = value + prbuf[chip].astype(jnp.float32)
        if k:
            sbuf[chip] = value.astype(jnp.bfloat16)
            send(sbuf.at[chip], rbuf.at[p], rsem.at[p], (g, chip * 2 + c))
        else:
            result = value
    for k in range(1, chips):
        chip = flip(p, k)
        pltpu.make_async_copy(rbuf.at[chip], rbuf.at[chip], rsem.at[chip]).wait()
        result = result + rbuf[chip].astype(jnp.float32)
    out[...] = result.astype(jnp.bfloat16)
    assert len(sends) == send_sem.shape[0]
    for copy, when in sends:
        if when is None:
            copy.wait_send()
        else:
            pl.when(when)(copy.wait_send)


def on_device(
    near,
    prompt_states,
    page_table,
    step_states,
    sample_order,
    key_weight,
    value_weight,
    query_weight,
    out_weight,
):
    groups = lax.axis_size("groups")
    devices = lax.axis_size("sample")
    chips = devices // 2
    own_chip = lax.axis_index("sample") // 2
    dim = prompt_states.shape[1]
    tokens = 2 * prompt_states.shape[0]
    chip_pages = tokens // PAGE
    heads = query_weight.shape[1] // HEAD_DIM
    total_pages = page_table.shape[0]
    prompts = total_pages // PROMPT_PAGES
    samples = sample_order.shape[0]
    wide = 2 * samples
    cols = dim // devices
    half = devices // 2
    lanes = heads * wide

    order = np.arange(HEAD_DIM) % (HEAD_DIM // 2)
    frequency = jnp.asarray((ROPE_BASE ** (-order * 2.0 / HEAD_DIM)).astype(np.float32))[None, :]
    deep = chips // near
    own_parts = groups // 2
    send_count = (
        CHUNKS * own_parts * (16 + 2 + 4 * (near - 1))
        + 2 * CHUNKS * (deep - 1) * near
        + 2 * CHUNKS * (deep - 2) * groups
        - 2 * CHUNKS * (deep - 2) * 1
        + 2 * CHUNKS * (deep - 1) * (near - 1) * (groups - 1)
        - 2 * CHUNKS * (deep - 1)
        + 2 * CHUNKS * (deep - 2)
        + 3 * chips
        + half
        + 1
    )
    masked = prompts > 1
    args = [
        prompt_states,
        step_states.reshape(wide, dim),
        key_weight,
        value_weight,
        query_weight,
        out_weight,
        page_table[None, :],
        frequency,
    ]
    specs = [pl.BlockSpec(memory_space=pl.ANY)] * 6 + [pl.BlockSpec(memory_space=pltpu.VMEM)] * 2
    if masked:
        page_ids = own_chip * chip_pages + jnp.arange(chip_pages, dtype=jnp.int32)
        slots = jnp.sum(
            jnp.where(
                page_table[None, :] == page_ids[:, None],
                jnp.arange(total_pages, dtype=jnp.int32)[None, :],
                0,
            ),
            axis=1,
        )
        token_prompt = jnp.repeat(slots // PROMPT_PAGES, PAGE)[:, None]
        query_prompt = jnp.tile(sample_order // (samples // prompts), 2 * heads)[None, :]
        args += [token_prompt, query_prompt]
        specs += [pl.BlockSpec(memory_space=pltpu.VMEM)] * 2
    bf16, f32 = jnp.bfloat16, jnp.float32
    dma = pltpu.SemaphoreType.DMA
    result = pl.pallas_call(
        functools.partial(kernel, (groups, devices, near, samples, heads, masked)),
        out_shape=jax.ShapeDtypeStruct((wide, cols), bf16),
        in_specs=specs,
        out_specs=pl.BlockSpec(memory_space=pltpu.VMEM),
        scratch_shapes=[
            pltpu.VMEM((tokens + wide, HEAD_DIM), f32),
            pltpu.VMEM((tokens + wide, HEAD_DIM), f32),
            pltpu.VMEM((tokens + wide, dim), bf16),
            pltpu.VMEM((dim, 2 * HALF), bf16),
            pltpu.VMEM((dim, heads * HEAD_DIM), bf16),
            pltpu.VMEM((heads * HEAD_DIM, dim), bf16),
            pltpu.VMEM((tokens + wide, 2 * HALF), f32),
            pltpu.VMEM((2, tokens + wide, HEAD_DIM), bf16),
            pltpu.VMEM((2, tokens + wide, HEAD_DIM), bf16),
            pltpu.VMEM((lanes, HEAD_DIM), bf16),
            pltpu.VMEM((half, lanes, HEAD_DIM), bf16),
            pltpu.VMEM((half, HEAD_DIM + TAIL, lanes), bf16),
            pltpu.VMEM((chips, HEAD_DIM + TAIL, lanes), bf16),
            pltpu.VMEM((2, wide, HEAD_DIM), bf16),
            pltpu.VMEM((2, wide, HEAD_DIM), bf16),
            pltpu.VMEM((chips, wide, cols), bf16),
            pltpu.VMEM((chips, wide, cols), bf16),
            pltpu.VMEM((chips, wide, cols), bf16),
            pltpu.VMEM((chips, wide, cols), bf16),
            dma((6,)),
            dma((send_count,)),
            dma((chips * groups * CHUNKS,)),
            dma,
            dma((half,)),
            dma((chips,)),
            dma,
            dma((chips,)),
            dma((chips,)),
        ],
        compiler_params=pltpu.CompilerParams(
            collective_id=0, has_side_effects=True, vmem_limit_bytes=60 * 1024 * 1024
        ),
        name="prefill_decode",
    )(*args)
    return result.reshape(2, samples, cols)


def solution(mesh):
    in_specs = (
        P(("groups", "sample"), None),
        P("groups"),
        P(None, "groups", None),
        P("groups"),
        P("sample", None),
        P("sample", None),
        P(None, "sample"),
        P("sample", None),
    )
    out_specs = P(None, "groups", "sample")
    near = 2 if mesh.shape["groups"] == 2 else 1
    return jax.shard_map(
        functools.partial(on_device, near), mesh=mesh, in_specs=in_specs, out_specs=out_specs,
        check_vma=False,
    )
```
